32 devices in a mesh: ep: 8 (over z, x), rep: 4 (over y, core).
Axes of the slice: x: 2, y: 2, z: 4, core: 2. Of those that a mesh axis runs over, the one named last changes fastest.
Arguments:
- tokens: bfloat16 [4096, 4096], P(('ep', 'rep')), may hold values from -6 to 6
- expert_ids: int32 [4096, 2], P(('ep', 'rep')), may hold values from 0 to 63, as said below
- route_weights: float32 [4096, 2], P(('ep', 'rep')), may hold values from 0.1 to 1
- w_gate: bfloat16 [4, 4096, 2048], P('rep', None, 'ep'), may hold values from -0.09375 to 0.09375
- w_up: bfloat16 [4, 4096, 2048], P('rep', None, 'ep'), may hold values from -0.09375 to 0.09375
- w_down: bfloat16 [4, 2048, 4096], P('rep', 'ep'), may hold values from -0.125 to 0.125
- cotangent: bfloat16 [4096, 4096], P(('ep', 'rep')), may hold values from -6 to 6
Outputs:
- mixed: bfloat16 [4096, 4096], P(('ep', 'rep'))
- grad_tokens: bfloat16 [4096, 4096], P(('ep', 'rep'))
- grad_gate: bfloat16 [4, 4096, 2048], P('rep', None, 'ep')
- grad_up: bfloat16 [4, 4096, 2048], P('rep', None, 'ep')
- grad_down: bfloat16 [4, 2048, 4096], P('rep', 'ep')
The draws below stay inside these ranges and needn't reach their ends.
Inputs may be any that keep to these rules, and one draw needn't show every extreme that they name: `expert_ids`: A token's two experts differ. Among the rows of one device, each expert below 4 is named at most 4 times; one of them is named exactly 4 times by every device.
All inputs are finite; a program needn't handle non-finite values.
Results may differ from the reference program's by a relative error of at most 0.0058.
Values may be sent and summed in bfloat16 or wider, within the bound.
No kernel may reach another device: no remote copies, remote signals or barrier semaphores. Data moves between devices by JAX's collectives and lax.ppermute only.
A program may use at most 128 MiB of HBM per device.

```python
import jax
import jax.numpy as jnp
from jax import lax

D = 4096
EXPERTS_ALL = 64
TOK_DEV = 128
CAP = 4
FF = 2048
WIN = 4
TOKENS = 4096
DEVICES = 32


def draw_expert_ids(key, part):
    favored = jax.random.randint(jax.random.fold_in(key, 3), (), 0, WIN)
    outside = EXPERTS_ALL - WIN

    def one_block(index):
        block_key = jax.random.fold_in(jax.random.fold_in(key, 11), index)
        counts = jax.random.randint(jax.random.fold_in(block_key, 1), (WIN,), 1, CAP + 1)
        counts = jnp.where(jnp.arange(WIN, dtype=jnp.int32) == favored, CAP, counts)
        lanes = jnp.arange(WIN * CAP, dtype=jnp.int32)
        which = lanes // CAP
        valid = lanes % CAP < counts[which]
        chosen = jax.random.permutation(jax.random.fold_in(block_key, 2), TOK_DEV)[:WIN * CAP]
        inside = jnp.full((TOK_DEV,), -1, jnp.int32).at[chosen].set(jnp.where(valid, which, -1).astype(jnp.int32))
        first = jax.random.randint(jax.random.fold_in(block_key, 3), (TOK_DEV,), 0, outside)
        offset = jax.random.randint(jax.random.fold_in(block_key, 4), (TOK_DEV,), 1, outside)
        second = (first + offset) % outside
        column = jax.random.randint(jax.random.fold_in(block_key, 5), (TOK_DEV,), 0, 2)
        left = jnp.where((inside >= 0) & (column == 0), inside, first + WIN)
        right = jnp.where((inside >= 0) & (column == 1), inside, second + WIN)
        return jnp.stack([left, right], axis=1).astype(jnp.int32)
    return lax.map(one_block, jnp.arange(DEVICES, dtype=jnp.int32)).reshape(TOKENS, 2)


def steps_of(key, extent, cuts, low, top_value):
    factor_of, own = 1.0, jax.random.fold_in(key, 6)
    for dim, blocks in cuts:
        steps = jnp.exp(jax.random.uniform(jax.random.fold_in(own, dim), (blocks,), jnp.float32, low / len(cuts), top_value / len(cuts)))
        factor_of = factor_of * jnp.repeat(steps, extent[dim] // blocks).reshape([-1 if axis == dim else 1 for axis in range(len(extent))])
    return factor_of


def scatter_about(rng, extent, spread, limit, shards=(), held_as=jnp.bfloat16):
    level = steps_of(rng, extent, shards, -0.22, 0.18) if shards else 1.0
    result = jax.random.normal(rng, extent, jnp.float32) * spread * level
    return jnp.minimum(jnp.maximum(result, -limit), limit).astype(held_as)


def setup_inputs(seed: int = 0) -> dict:
    streams_of = jax.random.split(jax.random.key(seed), 8)
    return {
        "tokens": scatter_about(streams_of[0], (TOKENS, D), 1.0, 6.0, ((0, 32),)),
        "expert_ids": draw_expert_ids(jax.random.fold_in(streams_of[7], 71), 0),
        "route_weights": jnp.clip(0.1 + 0.9 * jax.random.uniform(streams_of[2], (TOKENS, 2), jnp.float32) ** steps_of(streams_of[2], (TOKENS, 2), ((0, 32),), -0.2, 0.2), 0.1, 1.0),
        "w_gate": scatter_about(streams_of[3], (WIN, D, FF), D ** -0.5, 0.09375, ((0, 4), (2, 8))),
        "w_up": scatter_about(streams_of[4], (WIN, D, FF), D ** -0.5, 0.09375, ((0, 4), (2, 8))),
        "w_down": scatter_about(streams_of[5], (WIN, FF, D), FF ** -0.5, 0.125, ((0, 4), (1, 8))),
        "cotangent": scatter_about(streams_of[6], (TOKENS, D), 1.0, 6.0, ((0, 32),)),
    }


def reference(tokens, expert_ids, route_weights, w_gate, w_up, w_down, cotangent):
    routes = TOKENS * 2
    most = DEVICES * CAP
    flat_e = expert_ids.reshape(-1)
    bucket = jnp.minimum(flat_e, WIN).astype(jnp.int32)
    order = jnp.argsort(bucket, stable=True).astype(jnp.int32)
    counts = jax.ops.segment_sum(jnp.ones((routes,), jnp.int32), bucket, num_segments=WIN + 1)
    starts = (jnp.cumsum(counts) - counts).astype(jnp.int32)
    order_pad = jnp.concatenate([order, jnp.zeros((most,), jnp.int32)])
    flat_weights = route_weights.reshape(-1)
    lanes = jnp.arange(most, dtype=jnp.int32)

    def per_expert(carry, inputs):
        mixed_acc, grad_acc = carry
        wg, wu, wd, expert = inputs
        picked = lax.dynamic_slice(order_pad, (starts[expert].astype(jnp.int32),), (most,))
        valid = lanes < counts[expert]
        token_of = picked // 2
        weight = jnp.where(valid, flat_weights[picked], 0.0)
        rows = jnp.where(valid[:, None], tokens[token_of], jnp.zeros((), jnp.bfloat16))
        pre_gate = jnp.dot(rows, wg, preferred_element_type=jnp.float32)
        pre_up = jnp.dot(rows, wu, preferred_element_type=jnp.float32)
        logistic = jax.nn.sigmoid(pre_gate)
        activated = pre_gate * logistic
        hidden = (activated * pre_up).astype(jnp.bfloat16)
        routed = jnp.dot(hidden, wd, preferred_element_type=jnp.float32).astype(jnp.bfloat16)
        mixed_acc = mixed_acc.at[token_of].add(weight[:, None] * routed.astype(jnp.float32))
        upstream = (weight[:, None] * cotangent[token_of].astype(jnp.float32)).astype(jnp.bfloat16)
        d_act = jnp.dot(upstream, wd.T, preferred_element_type=jnp.float32)
        d_up = (d_act * activated).astype(jnp.bfloat16)
        d_gate = (d_act * pre_up * logistic * (1.0 + pre_gate * (1.0 - logistic))).astype(jnp.bfloat16)
        grad_sum = jnp.dot(d_gate, wg.T, preferred_element_type=jnp.float32) + jnp.dot(d_up, wu.T, preferred_element_type=jnp.float32)
        route_grad = grad_sum.astype(jnp.bfloat16)
        grad_acc = grad_acc.at[token_of].add(jnp.where(valid[:, None], route_grad.astype(jnp.float32), 0.0))
        part_gate = jnp.dot(rows.T, d_gate, preferred_element_type=jnp.float32).astype(jnp.bfloat16)
        part_up = jnp.dot(rows.T, d_up, preferred_element_type=jnp.float32).astype(jnp.bfloat16)
        part_down = jnp.dot(hidden.T, upstream, preferred_element_type=jnp.float32).astype(jnp.bfloat16)
        return (mixed_acc, grad_acc), (part_gate, part_up, part_down)

    begin = (jnp.zeros((TOKENS, D), jnp.float32), jnp.zeros((TOKENS, D), jnp.float32))
    (mixed_acc, grad_acc), grads = lax.scan(per_expert, begin, (w_gate, w_up, w_down, jnp.arange(WIN, dtype=jnp.int32)))
    return mixed_acc.astype(jnp.bfloat16), grad_acc.astype(jnp.bfloat16), grads[0], grads[1], grads[2]
```

```python
import jax
import jax.numpy as jnp
from jax import lax
from jax.experimental import pallas as pl
from jax.experimental.pallas import tpu as pltpu
from jax.sharding import PartitionSpec as P

CAP = 4
BF = jnp.bfloat16
F32 = jnp.float32
VMEM = pl.BlockSpec(memory_space=pltpu.VMEM)
SMEM = pl.BlockSpec(memory_space=pltpu.SMEM)


def call(body, out_shape, n_in, limit=24, smem=0):
    return pl.pallas_call(
        body,
        out_shape=out_shape,
        in_specs=[SMEM] * smem + [VMEM] * (n_in - smem),
        out_specs=jax.tree.map(lambda _: VMEM, out_shape),
        compiler_params=pltpu.CompilerParams(vmem_limit_bytes=limit << 20),
    )


def selection(rank_id, ids, n_rep):
    slots = n_rep * CAP
    tok = ids.shape[1]
    row = lax.broadcasted_iota(jnp.int32, (slots, tok), 0)
    expert = jnp.bitwise_xor(rank_id, row // CAP)
    first = ids[0:1, :] == expert
    second = ids[1:2, :] == expert
    member = jnp.logical_or(first, second)
    below = lax.broadcasted_iota(jnp.int32, (tok, tok), 0) < lax.broadcasted_iota(
        jnp.int32, (tok, tok), 1
    )
    earlier = jnp.dot(
        jnp.where(member, 1.0, 0.0).astype(BF),
        jnp.where(below, 1.0, 0.0).astype(BF),
        preferred_element_type=F32,
    )
    chosen = jnp.logical_and(member, earlier == (row % CAP).astype(F32))
    return chosen, first


def slot_weights(chosen, first, weights):
    both = jnp.where(first, weights[0:1, :], weights[1:2, :])
    return jnp.sum(jnp.where(chosen, both, 0.0), axis=1, keepdims=True)


def pack(rank_id, ids, weights, tokens, cotangent, n_rep):
    width = tokens.shape[1]

    def body(rank_ref, ids_ref, weights_ref, tokens_ref, cotangent_ref, *outs):
        chosen, first = selection(rank_ref[0], ids_ref[...], n_rep)
        scale = slot_weights(chosen, first, weights_ref[...])
        pick = jnp.where(chosen, 1.0, 0.0).astype(BF)
        rows = jnp.dot(pick, tokens_ref[...], preferred_element_type=F32)
        ups = jnp.dot(pick, cotangent_ref[...], preferred_element_type=F32) * scale
        for k in range(n_rep):
            outs[k][0:CAP, :] = rows[k * CAP : (k + 1) * CAP].astype(BF)
            outs[k][CAP : 2 * CAP, :] = ups[k * CAP : (k + 1) * CAP].astype(BF)

    shape = [jax.ShapeDtypeStruct((2 * CAP, width), BF)] * n_rep
    return call(body, shape, 5, smem=1)(rank_id, ids, weights, tokens, cotangent)


def split_blocks(blocks):
    n = len(blocks)
    width = blocks[0].shape[1]

    def body(*refs):
        ins, (tok_ref, up_ref) = refs[:n], refs[n:]
        tok_ref[...] = jnp.concatenate([r[0:CAP, :] for r in ins], axis=0)
        up_ref[...] = jnp.concatenate([r[CAP : 2 * CAP, :] for r in ins], axis=0)

    shape = [jax.ShapeDtypeStruct((n * CAP, width), BF)] * 2
    return call(body, shape, n)(*blocks)


def unpack_mixed(rank_id, ids, weights, blocks):
    n = len(blocks)
    width = blocks[0].shape[1]
    tok = ids.shape[1]

    def body(rank_ref, ids_ref, weights_ref, *refs):
        ins, out_ref = refs[:n], refs[n]
        chosen, first = selection(rank_ref[0], ids_ref[...], n)
        scale = slot_weights(chosen, first, weights_ref[...])
        pick = jnp.where(chosen, 1.0, 0.0).astype(BF)
        rows = jnp.concatenate([r[...].astype(F32) for r in ins], axis=0) * scale
        top = rows.astype(BF)
        rest = rows - top.astype(F32)
        middle = rest.astype(BF)
        low = (rest - middle.astype(F32)).astype(BF)
        out_ref[...] = lax.dot_general(
            jnp.concatenate([pick, pick, pick], axis=0),
            jnp.concatenate([top, middle, low], axis=0),
            (((0,), (0,)), ((), ())),
            preferred_element_type=F32,
        ).astype(BF)

    return call(body, jax.ShapeDtypeStruct((tok, width), BF), 3 + n, smem=1)(
        rank_id, ids, weights, *blocks
    )


def unpack_grads(rank_id, ids, blocks):
    n = len(blocks)
    width = blocks[0].shape[1]
    tok = ids.shape[1]

    def body(rank_ref, ids_ref, *refs):
        ins, out_ref = refs[:n], refs[n]
        chosen, _ = selection(rank_ref[0], ids_ref[...], n)
        pick = jnp.where(chosen, 1.0, 0.0).astype(BF)
        rows = jnp.concatenate([r[...] for r in ins], axis=0)
        out_ref[...] = lax.dot_general(
            pick, rows, (((0,), (0,)), ((), ())), preferred_element_type=F32
        ).astype(BF)

    return call(body, jax.ShapeDtypeStruct((tok, width), BF), 2 + n, smem=1)(
        rank_id, ids, *blocks
    )


def part_types(n, rows, width, heavy):
    half = n // 2
    starts = {half, n - half + 1} if heavy > 0 else {half, half - 1}
    return [
        jax.ShapeDtypeStruct((rows, width), BF if d in starts else F32) for d in range(n)
    ]


def forward(chunks, w_gate, w_up, w_down, heavy):
    n = len(chunks)
    rows, width = chunks[0].shape
    ff = w_gate.shape[1]
    total = n * rows

    def body(*refs):
        ins, (wg, wu, wd) = refs[:n], refs[n : n + 3]
        all_ref, hidden_ref, act_ref, slope_ref = refs[n + 3 : n + 7]
        outs = refs[n + 7 :]
        for d in range(n):
            all_ref[d * rows : (d + 1) * rows, :] = ins[d][...]
        x = all_ref[...]
        pre_gate = jnp.dot(x, wg[...], preferred_element_type=F32)
        pre_up = jnp.dot(x, wu[...], preferred_element_type=F32)
        logistic = jax.nn.sigmoid(pre_gate)
        activated = pre_gate * logistic
        hidden = (activated * pre_up).astype(BF)
        hidden_ref[...] = hidden
        act_ref[...] = activated
        slope_ref[...] = pre_up * logistic * (1.0 + pre_gate * (1.0 - logistic))
        routed = jnp.dot(hidden, wd[...], preferred_element_type=F32)
        for d in range(n):
            outs[d][...] = routed[d * rows : (d + 1) * rows].astype(outs[d].dtype)

    shape = [
        jax.ShapeDtypeStruct((total, width), BF),
        jax.ShapeDtypeStruct((total, ff), BF),
        jax.ShapeDtypeStruct((total, ff), F32),
        jax.ShapeDtypeStruct((total, ff), F32),
    ] + part_types(n, rows, width, heavy)
    out = call(body, shape, n + 3, limit=40)(*chunks, w_gate, w_up, w_down)
    return out[0], out[1], out[2], out[3], out[4:]


def backward(chunks, activated, slope, w_gate, w_up, w_down, heavy):
    n = len(chunks)
    rows, width = chunks[0].shape
    ff = w_gate.shape[1]
    total = n * rows
    across = (((1,), (1,)), ((), ()))

    def body(*refs):
        ins, (act_ref, slope_ref, wg, wu, wd) = refs[:n], refs[n : n + 5]
        all_ref, dg_ref, du_ref = refs[n + 5 : n + 8]
        outs = refs[n + 8 :]
        for d in range(n):
            all_ref[d * rows : (d + 1) * rows, :] = ins[d][...]
        d_act = lax.dot_general(all_ref[...], wd[...], across, preferred_element_type=F32)
        d_up = (d_act * act_ref[...]).astype(BF)
        d_gate = (d_act * slope_ref[...]).astype(BF)
        dg_ref[...] = d_gate
        du_ref[...] = d_up
        grads = lax.dot_general(d_gate, wg[...], across, preferred_element_type=F32)
        grads += lax.dot_general(d_up, wu[...], across, preferred_element_type=F32)
        for d in range(n):
            outs[d][...] = grads[d * rows : (d + 1) * rows].astype(outs[d].dtype)

    shape = [
        jax.ShapeDtypeStruct((total, width), BF),
        jax.ShapeDtypeStruct((total, ff), BF),
        jax.ShapeDtypeStruct((total, ff), BF),
    ] + part_types(n, rows, width, heavy)
    out = call(body, shape, n + 5, limit=40)(*chunks, activated, slope, w_gate, w_up, w_down)
    return out[0], out[1], out[2], out[3:]


def ring_order(n):
    return [i for i in range(0, n, 2)] + [i for i in reversed(range(1, n, 2))]


def shift(value, step):
    n = lax.axis_size("ep")
    order = ring_order(n)
    return lax.ppermute(value, "ep", [(order[i], order[(i + step) % n]) for i in range(n)])


def ring_gather(chunk, heavy):
    n = lax.axis_size("ep")
    half = n // 2
    found = {0: chunk}
    ahead = behind = chunk
    for step in range(1, half + 1):
        ahead = shift(ahead, heavy)
        found[(-heavy * step) % n] = ahead
        if step < half:
            behind = shift(behind, -heavy)
            found[(heavy * step) % n] = behind
    return [found[d] for d in range(n)]


def ring_scatter(parts, heavy):
    n = len(parts)
    half = n // 2
    ahead = shift(parts[half], heavy)
    behind = shift(parts[(-heavy * (half - 1)) % n], -heavy)
    for step in range(1, half):
        d = (heavy * (half - step)) % n
        ahead = shift((ahead.astype(F32) + parts[d]).astype(BF), heavy)
        if step < half - 1:
            d = (-heavy * (half - 1 - step)) % n
            behind = shift((behind.astype(F32) + parts[d]).astype(BF), -heavy)
    return parts[0], ahead, behind


def finish(own, ahead, behind, n):
    width = own.shape[1]

    def body(own_ref, ahead_ref, behind_ref, *outs):
        total = own_ref[...] + ahead_ref[...].astype(F32) + behind_ref[...].astype(F32)
        for k in range(n):
            outs[k][...] = total[k * CAP : (k + 1) * CAP].astype(BF)

    shape = [jax.ShapeDtypeStruct((CAP, width), BF)] * n
    return call(body, shape, 3)(own, ahead, behind)


def trade(blocks):
    n = lax.axis_size("rep")
    return [blocks[0]] + [
        lax.ppermute(blocks[k], "rep", [(i, i ^ k) for i in range(n)]) for k in range(1, n)
    ]


def local(tokens, expert_ids, route_weights, w_gate, w_up, w_down, cotangent):
    n_rep = lax.axis_size("rep")
    rank_id = lax.axis_index("rep").astype(jnp.int32).reshape(1)
    ids = expert_ids.T
    weights = route_weights.T
    wg, wu, wd = w_gate[0], w_up[0], w_down[0]
    blocks = trade(pack(rank_id, ids, weights, tokens, cotangent, n_rep))
    token_rows, up_rows = split_blocks(blocks)
    token_chunks = ring_gather(token_rows, 1)
    up_chunks = ring_gather(up_rows, -1)
    all_tokens, hidden, activated, slope, routed_parts = forward(token_chunks, wg, wu, wd, 1)
    routed = ring_scatter(routed_parts, 1)
    all_ups, d_gate, d_up, grad_parts = backward(up_chunks, activated, slope, wg, wu, wd, -1)
    row_grads = ring_scatter(grad_parts, -1)
    over_rows = (((0,), (0,)), ((), ()))

    def weight_grad(left, right):
        return lax.dot_general(left, right, over_rows, preferred_element_type=F32).astype(BF)[None]

    grad_gate = weight_grad(all_tokens, d_gate)
    grad_up = weight_grad(all_tokens, d_up)
    grad_down = weight_grad(hidden, all_ups)
    mixed = unpack_mixed(rank_id, ids, weights, trade(finish(*routed, n_rep)))
    grad_tokens = unpack_grads(rank_id, ids, trade(finish(*row_grads, n_rep)))
    return (mixed, grad_tokens, grad_gate, grad_up, grad_down)


def solution(mesh):
    placed = (
        P(("ep", "rep"), None),
        P(("ep", "rep"), None),
        P(("ep", "rep"), None),
        P("rep", None, "ep"),
        P("rep", None, "ep"),
        P("rep", "ep", None),
        P(("ep", "rep"), None),
    )
    return jax.shard_map(
        local,
        mesh=mesh,
        in_specs=placed,
        out_specs=(
            P(("ep", "rep"), None),
            P(("ep", "rep"), None),
            P("rep", None, "ep"),
            P("rep", None, "ep"),
            P("rep", "ep", None),
        ),
        check_vma=False,
    )
```

```python
import jax
import jax.numpy as jnp
from jax import lax
from jax.experimental import pallas as pl
from jax.experimental.pallas import tpu as pltpu
from jax.sharding import PartitionSpec as P


CAP = 4
BF = jnp.bfloat16
F32 = jnp.float32
VMEM = pl.BlockSpec(memory_space=pltpu.VMEM)
SMEM = pl.BlockSpec(memory_space=pltpu.SMEM)
HBM = pl.BlockSpec(memory_space=pltpu.HBM)


def call(body, out_shape, n_in, limit=12, smem=0):
    return pl.pallas_call(
        body,
        out_shape=out_shape,
        in_specs=[SMEM] * smem + [VMEM] * (n_in - smem),
        out_specs=jax.tree.map(lambda _: VMEM, out_shape),
        compiler_params=pltpu.CompilerParams(vmem_limit_bytes=limit << 20),
    )


def selection(rank_id, ids, n_rep):
    slots = n_rep * CAP
    tok = ids.shape[1]
    row = lax.broadcasted_iota(jnp.int32, (slots, tok), 0)
    expert = jnp.bitwise_xor(rank_id, row // CAP)
    first = ids[0:1, :] == expert
    second = ids[1:2, :] == expert
    member = jnp.logical_or(first, second)
    below = lax.broadcasted_iota(jnp.int32, (tok, tok), 0) < lax.broadcasted_iota(
        jnp.int32, (tok, tok), 1
    )
    earlier = jnp.dot(
        jnp.where(member, 1.0, 0.0).astype(BF),
        jnp.where(below, 1.0, 0.0).astype(BF),
        preferred_element_type=F32,
    )
    chosen = jnp.logical_and(member, earlier == (row % CAP).astype(F32))
    return chosen, first


def slot_weights(chosen, first, weights):
    both = jnp.where(first, weights[0:1, :], weights[1:2, :])
    return jnp.sum(jnp.where(chosen, both, 0.0), axis=1, keepdims=True)


def in_hbm(arrays):
    return [pltpu.with_memory_space_constraint(v, pltpu.HBM) for v in arrays]


def pack(rank_id, ids, weights, tokens, cotangent, n_rep):
    width = tokens.shape[1]
    given = [ids, weights, tokens, cotangent]

    def body(rank_ref, *refs):
        ins, outs = refs[:4], refs[4 : 4 + n_rep]
        held, sems = refs[4 + n_rep : 8 + n_rep], refs[-1]
        copies = [
            pltpu.make_async_copy(src, dst, sems.at[i])
            for i, (src, dst) in enumerate(zip(ins, held))
        ]
        for copy in copies:
            copy.start()
        copies[0].wait()
        copies[1].wait()
        chosen, first = selection(rank_ref[0], held[0][...], n_rep)
        scale = slot_weights(chosen, first, held[1][...])
        pick = jnp.where(chosen, 1.0, 0.0).astype(BF)
        copies[2].wait()
        rows = jnp.dot(pick, held[2][...], preferred_element_type=F32)
        for k in range(n_rep):
            outs[k][0:CAP, :] = rows[k * CAP : (k + 1) * CAP].astype(BF)
        copies[3].wait()
        rows = jnp.dot(pick, held[3][...], preferred_element_type=F32) * scale
        for k in range(n_rep):
            outs[k][CAP : 2 * CAP, :] = rows[k * CAP : (k + 1) * CAP].astype(BF)

    return pl.pallas_call(
        body,
        out_shape=[jax.ShapeDtypeStruct((2 * CAP, width), BF)] * n_rep,
        in_specs=[SMEM] + [HBM] * 4,
        out_specs=[VMEM] * n_rep,
        scratch_shapes=[pltpu.VMEM(v.shape, v.dtype) for v in given]
        + [pltpu.SemaphoreType.DMA((4,))],
        compiler_params=pltpu.CompilerParams(vmem_limit_bytes=12 << 20),
    )(rank_id, *in_hbm(given))


def load(*arrays):
    n = len(arrays)

    def body(*refs):
        ins, outs, turned, sems = refs[:n], refs[n : 2 * n], refs[2 * n : 3 * n], refs[3 * n]
        copies = [pltpu.make_async_copy(ins[i], outs[i], sems.at[i]) for i in range(n)]
        for copy in copies:
            copy.start()
        for i in range(n):
            copies[i].wait()
            turned[i][...] = outs[i][...].T

    out = pl.pallas_call(
        body,
        out_shape=[jax.ShapeDtypeStruct(a.shape, a.dtype) for a in arrays]
        + [jax.ShapeDtypeStruct(a.shape[::-1], a.dtype) for a in arrays],
        in_specs=[HBM] * n,
        out_specs=[VMEM] * (2 * n),
        scratch_shapes=[pltpu.SemaphoreType.DMA((n,))],
        compiler_params=pltpu.CompilerParams(vmem_limit_bytes=12 << 20),
    )(*in_hbm(arrays))
    return out[:n], out[n:]


def split(blocks):
    n = len(blocks)
    width = blocks[0].shape[1]

    def body(*refs):
        ins, (tok_ref, up_ref) = refs[:n], refs[n:]
        tok_ref[...] = jnp.concatenate([r[0:CAP, :] for r in ins], axis=0)
        up_ref[...] = jnp.concatenate([r[CAP : 2 * CAP, :] for r in ins], axis=0)

    shape = [jax.ShapeDtypeStruct((n * CAP, width), BF)] * 2
    return call(body, shape, n)(*blocks)


def streamed(compute, tiles, out_shapes, n_in, smem=0):
    n_out = len(out_shapes)

    def body(*refs):
        ins, outs = refs[:n_in], refs[n_in : n_in + n_out]
        held, sems = refs[n_in + n_out : n_in + 2 * n_out], refs[-1]
        copies = []
        state = None
        for i in range(tiles):
            state, results = compute(ins, i, state)
            for j, (where, value) in enumerate(results):
                held[j][where] = value.astype(BF)
                copy = pltpu.make_async_copy(
                    held[j].at[where], outs[j].at[where], sems.at[i * n_out + j]
                )
                copy.start()
                copies.append(copy)
        for copy in copies:
            copy.wait()

    return pl.pallas_call(
        body,
        out_shape=[jax.ShapeDtypeStruct(shape, BF) for shape in out_shapes],
        in_specs=[SMEM] * smem + [VMEM] * (n_in - smem),
        out_specs=[HBM] * n_out,
        scratch_shapes=[pltpu.VMEM(shape, BF) for shape in out_shapes]
        + [pltpu.SemaphoreType.DMA((tiles * n_out,))],
        compiler_params=pltpu.CompilerParams(vmem_limit_bytes=24 << 20),
    )


OVER_ROWS = (((0,), (0,)), ((), ()))


def unpack(rank_id, ids, weights, blocks):
    n = len(blocks)
    width = blocks[0].shape[1]
    tok = ids.shape[1]
    tiles = 4
    cols = width // tiles

    def compute(ins, i, state):
        at = slice(i * cols, (i + 1) * cols)
        if state is None:
            chosen, first = selection(ins[0][0], ins[1][...], n)
            pick = jnp.where(chosen, 1.0, 0.0).astype(BF)
            state = (pick, slot_weights(chosen, first, ins[2][...]))
        pick, scale = state
        full = jnp.concatenate([r[0:CAP, at].astype(F32) for r in ins[3:]], axis=0) * scale
        top = full.astype(BF)
        rest = full - top.astype(F32)
        middle = rest.astype(BF)
        low = (rest - middle.astype(F32)).astype(BF)
        mixed = lax.dot_general(
            jnp.concatenate([pick, pick, pick], axis=0),
            jnp.concatenate([top, middle, low], axis=0),
            OVER_ROWS,
            preferred_element_type=F32,
        )
        rows = jnp.concatenate([r[CAP : 2 * CAP, at] for r in ins[3:]], axis=0)
        grads = lax.dot_general(pick, rows, OVER_ROWS, preferred_element_type=F32)
        return state, [((slice(None), at), mixed), ((slice(None), at), grads)]

    kernel = streamed(compute, tiles, [(tok, width)] * 2, 3 + n, smem=1)
    return kernel(rank_id, ids, weights, *blocks)


def weight_grads(*jobs):
    count = len(jobs)
    shapes = [(left.shape[1], right.shape[1]) for left, right in jobs]
    flat = [v for job in jobs for v in job]
    tiles = 4

    def body(*refs):
        ins, outs = refs[: 2 * count], refs[2 * count : 3 * count]
        held, sems = refs[3 * count : 4 * count], refs[-1]
        copies = []
        for j, (m, n) in enumerate(shapes):
            left, right = ins[2 * j], ins[2 * j + 1]
            for i in range(tiles):
                if m > n:
                    at = (slice(i * m // tiles, (i + 1) * m // tiles), slice(None))
                else:
                    at = (slice(None), slice(i * n // tiles, (i + 1) * n // tiles))
                held[j][at] = lax.dot_general(
                    left[:, at[0]], right[:, at[1]], OVER_ROWS, preferred_element_type=F32
                ).astype(BF)
                copy = pltpu.make_async_copy(held[j].at[at], outs[j].at[at], sems.at[j * tiles + i])
                copy.start()
                copies.append(copy)
        for copy in copies:
            copy.wait()

    return pl.pallas_call(
        body,
        out_shape=[jax.ShapeDtypeStruct(shape, BF) for shape in shapes],
        in_specs=[VMEM] * (2 * count),
        out_specs=[HBM] * count,
        scratch_shapes=[pltpu.VMEM(shape, BF) for shape in shapes]
        + [pltpu.SemaphoreType.DMA((tiles * count,))],
        compiler_params=pltpu.CompilerParams(vmem_limit_bytes=24 << 20),
    )(*flat)


def part_types(n, rows, width, heavy):
    half = n // 2
    starts = {half, n - half + 1} if heavy > 0 else {half, half - 1}
    return [
        jax.ShapeDtypeStruct((rows, width), BF if d in starts else F32) for d in range(n)
    ]


def forward(chunks, w_gate, w_up, w_down, heavy):
    n = len(chunks)
    rows, width = chunks[0].shape
    ff = w_gate.shape[1]
    total = n * rows

    def body(*refs):
        ins, (wg, wu, wd) = refs[:n], refs[n : n + 3]
        all_ref, hidden_ref, act_ref, slope_ref = refs[n + 3 : n + 7]
        outs = refs[n + 7 :]
        for d in range(n):
            all_ref[d * rows : (d + 1) * rows, :] = ins[d][...]
        x = all_ref[...]
        pre_gate = jnp.dot(x, wg[...], preferred_element_type=F32)
        pre_up = jnp.dot(x, wu[...], preferred_element_type=F32)
        logistic = jax.nn.sigmoid(pre_gate)
        activated = pre_gate * logistic
        hidden = (activated * pre_up).astype(BF)
        hidden_ref[...] = hidden
        act_ref[...] = activated
        slope_ref[...] = pre_up * logistic * (1.0 + pre_gate * (1.0 - logistic))
        routed = jnp.dot(hidden, wd[...], preferred_element_type=F32)
        for d in range(n):
            outs[d][...] = routed[d * rows : (d + 1) * rows].astype(outs[d].dtype)

    shape = [
        jax.ShapeDtypeStruct((total, width), BF),
        jax.ShapeDtypeStruct((total, ff), BF),
        jax.ShapeDtypeStruct((total, ff), F32),
        jax.ShapeDtypeStruct((total, ff), F32),
    ] + part_types(n, rows, width, heavy)
    out = call(body, shape, n + 3, limit=24)(*chunks, w_gate, w_up, w_down)
    return out[0], out[1], out[2], out[3], out[4:]


def backward(chunks, activated, slope, gate_t, up_t, down_t, heavy):
    n = len(chunks)
    rows, width = chunks[0].shape
    ff = gate_t.shape[0]
    total = n * rows

    def body(*refs):
        ins, (act_ref, slope_ref, wgt, wut, wdt) = refs[:n], refs[n : n + 5]
        all_ref, dg_ref, du_ref = refs[n + 5 : n + 8]
        outs = refs[n + 8 :]
        for d in range(n):
            all_ref[d * rows : (d + 1) * rows, :] = ins[d][...]
        d_act = jnp.dot(all_ref[...], wdt[...], preferred_element_type=F32)
        d_up = (d_act * act_ref[...]).astype(BF)
        d_gate = (d_act * slope_ref[...]).astype(BF)
        dg_ref[...] = d_gate
        du_ref[...] = d_up
        grads = jnp.dot(d_gate, wgt[...], preferred_element_type=F32)
        grads += jnp.dot(d_up, wut[...], preferred_element_type=F32)
        for d in range(n):
            outs[d][...] = grads[d * rows : (d + 1) * rows].astype(outs[d].dtype)

    shape = [
        jax.ShapeDtypeStruct((total, width), BF),
        jax.ShapeDtypeStruct((total, ff), BF),
        jax.ShapeDtypeStruct((total, ff), BF),
    ] + part_types(n, rows, width, heavy)
    out = call(body, shape, n + 5, limit=24)(*chunks, activated, slope, gate_t, up_t, down_t)
    return out[0], out[1], out[2], out[3:]


def ring_order(n):
    return [i for i in range(0, n, 2)] + [i for i in reversed(range(1, n, 2))]


def shift(value, step):
    n, n_rep = lax.axis_size("ep"), lax.axis_size("rep")
    order = ring_order(n)
    pairs = []
    for r in range(n_rep):
        way = step
        pairs += [
            (order[i] * n_rep + r, order[(i + way) % n] * n_rep + r) for i in range(n)
        ]
    return lax.ppermute(value, ("ep", "rep"), pairs)


def ring_gather(chunk, heavy):
    n = lax.axis_size("ep")
    half = n // 2
    found = {0: chunk}
    ahead = behind = chunk
    for step in range(1, half + 1):
        ahead = shift(ahead, heavy)
        found[(-heavy * step) % n] = ahead
        if step < half:
            behind = shift(behind, -heavy)
            found[(heavy * step) % n] = behind
    return [found[d] for d in range(n)]


def ring_scatter(parts, heavy):
    n = len(parts)
    half = n // 2
    ahead = shift(parts[half], heavy)
    behind = shift(parts[(-heavy * (half - 1)) % n], -heavy)
    for step in range(1, half):
        d = (heavy * (half - step)) % n
        ahead = shift((ahead.astype(F32) + parts[d]).astype(BF), heavy)
        if step < half - 1:
            d = (-heavy * (half - 1 - step)) % n
            behind = shift((behind.astype(F32) + parts[d]).astype(BF), -heavy)
    return parts[0], ahead, behind


def finish(routed, row_grads, n):
    width = routed[0].shape[1]

    def body(*refs):
        ins, outs = refs[:6], refs[6:]
        for half in range(2):
            own, ahead, behind = ins[3 * half : 3 * half + 3]
            total = own[...] + ahead[...].astype(F32) + behind[...].astype(F32)
            for k in range(n):
                outs[k][half * CAP : (half + 1) * CAP, :] = total[k * CAP : (k + 1) * CAP].astype(BF)

    shape = [jax.ShapeDtypeStruct((2 * CAP, width), BF)] * n
    return call(body, shape, 6)(*routed, *row_grads)


def trade(blocks):
    n = lax.axis_size("rep")
    found = [blocks[0]]
    for k in range(1, n):
        found.append(lax.ppermute(blocks[k], "rep", [(i, i ^ k) for i in range(n)]))
    return found


def local(tokens, expert_ids, route_weights, w_gate, w_up, w_down, cotangent):
    n_rep = lax.axis_size("rep")
    rank_id = lax.axis_index("rep").astype(jnp.int32).reshape(1)
    ids = expert_ids.T
    weights = route_weights.T

    sent = pack(rank_id, ids, weights, tokens, cotangent, n_rep)
    token_rows, up_rows = split(trade(sent))
    plain, turned = load(w_gate[0], w_up[0], w_down[0])
    token_chunks = ring_gather(token_rows, 1)
    up_chunks = ring_gather(up_rows, -1)
    all_tokens, hidden, activated, slope, routed_parts = forward(token_chunks, *plain, 1)
    routed = ring_scatter(routed_parts, 1)
    all_ups, d_gate, d_up, grad_parts = backward(up_chunks, activated, slope, *turned, -1)
    row_grads = ring_scatter(grad_parts, -1)
    grad_gate, grad_up = weight_grads((all_tokens, d_gate), (all_tokens, d_up))
    (grad_down,) = weight_grads((hidden, all_ups))
    back = trade(finish(routed, row_grads, n_rep))
    mixed, grad_tokens = unpack(rank_id, ids, weights, back)
    return (mixed, grad_tokens, grad_gate[None], grad_up[None], grad_down[None])


def solution(mesh):
    placed = (
        P(("ep", "rep"), None),
        P(("ep", "rep"), None),
        P(("ep", "rep"), None),
        P("rep", None, "ep"),
        P("rep", None, "ep"),
        P("rep", "ep", None),
        P(("ep", "rep"), None),
    )

    return jax.shard_map(
        local,
        mesh=mesh,
        in_specs=placed,
        out_specs=(
            P(("ep", "rep"), None),
            P(("ep", "rep"), None),
            P("rep", None, "ep"),
            P("rep", None, "ep"),
            P("rep", "ep", None),
        ),
        check_vma=False,
    )
```

```python
import jax
import jax.numpy as jnp
from jax import lax
from jax.experimental import pallas as pl
from jax.experimental.pallas import tpu as pltpu
from jax.sharding import PartitionSpec as P


CAP = 4
BF = jnp.bfloat16
F32 = jnp.float32
VMEM = pl.BlockSpec(memory_space=pltpu.VMEM)
SMEM = pl.BlockSpec(memory_space=pltpu.SMEM)
HBM = pl.BlockSpec(memory_space=pltpu.HBM)


def call(body, out_shape, n_in, limit=12, smem=0):
    return pl.pallas_call(
        body,
        out_shape=out_shape,
        in_specs=[SMEM] * smem + [VMEM] * (n_in - smem),
        out_specs=jax.tree.map(lambda _: VMEM, out_shape),
        compiler_params=pltpu.CompilerParams(vmem_limit_bytes=limit << 20),
    )


def selection(rank_id, ids, n_rep):
    slots = n_rep * CAP
    tok = ids.shape[1]
    row = lax.broadcasted_iota(jnp.int32, (slots, tok), 0)
    expert = jnp.bitwise_xor(rank_id, row // CAP)
    first = ids[0:1, :] == expert
    second = ids[1:2, :] == expert
    member = jnp.logical_or(first, second)
    below = lax.broadcasted_iota(jnp.int32, (tok, tok), 0) < lax.broadcasted_iota(
        jnp.int32, (tok, tok), 1
    )
    earlier = jnp.dot(
        jnp.where(member, 1.0, 0.0).astype(BF),
        jnp.where(below, 1.0, 0.0).astype(BF),
        preferred_element_type=F32,
    )
    chosen = jnp.logical_and(member, earlier == (row % CAP).astype(F32))
    return chosen, first


def slot_weights(chosen, first, weights):
    both = jnp.where(first, weights[0:1, :], weights[1:2, :])
    return jnp.sum(jnp.where(chosen, both, 0.0), axis=1, keepdims=True)


def in_hbm(arrays):
    return [pltpu.with_memory_space_constraint(v, pltpu.HBM) for v in arrays]


def pack(rank_id, ids, weights, tokens, cotangent, n_rep):
    tok, width = tokens.shape
    slots = n_rep * CAP
    given = [ids, weights, tokens, cotangent]

    def body(rank_ref, *refs):
        ins, outs = refs[:4], refs[4 : 4 + 2 * n_rep]
        pick_ref, scale_ref = refs[4 + 2 * n_rep : 6 + 2 * n_rep]
        held, sems = refs[6 + 2 * n_rep : 10 + 2 * n_rep], refs[-1]
        copies = [
            pltpu.make_async_copy(src, dst, sems.at[i])
            for i, (src, dst) in enumerate(zip(ins, held))
        ]
        for copy in copies:
            copy.start()
        copies[0].wait()
        copies[1].wait()
        chosen, first = selection(rank_ref[0], held[0][...], n_rep)
        scale = slot_weights(chosen, first, held[1][...])
        pick = jnp.where(chosen, 1.0, 0.0).astype(BF)
        pick_ref[...] = pick
        scale_ref[...] = jnp.broadcast_to(scale, (slots, tok))
        copies[2].wait()
        rows = jnp.dot(pick, held[2][...], preferred_element_type=F32)
        for k in range(n_rep):
            outs[k][...] = rows[k * CAP : (k + 1) * CAP].astype(BF)
        copies[3].wait()
        rows = jnp.dot(pick, held[3][...], preferred_element_type=F32) * scale
        for k in range(n_rep):
            outs[n_rep + k][...] = rows[k * CAP : (k + 1) * CAP].astype(BF)

    out = pl.pallas_call(
        body,
        out_shape=[jax.ShapeDtypeStruct((CAP, width), BF)] * (2 * n_rep)
        + [jax.ShapeDtypeStruct((slots, tok), BF), jax.ShapeDtypeStruct((slots, tok), F32)],
        in_specs=[SMEM] + [HBM] * 4,
        out_specs=[VMEM] * (2 * n_rep + 2),
        scratch_shapes=[pltpu.VMEM(v.shape, v.dtype) for v in given]
        + [pltpu.SemaphoreType.DMA((4,))],
        compiler_params=pltpu.CompilerParams(vmem_limit_bytes=12 << 20),
    )(rank_id, *in_hbm(given))
    return out[:n_rep], out[n_rep : 2 * n_rep], out[-2], out[-1]


def load(array):
    def body(src, dst, turned, sem):
        copy = pltpu.make_async_copy(src, dst, sem)
        copy.start()
        copy.wait()
        turned[...] = dst[...].T

    return pl.pallas_call(
        body,
        out_shape=[
            jax.ShapeDtypeStruct(array.shape, array.dtype),
            jax.ShapeDtypeStruct(array.shape[::-1], array.dtype),
        ],
        in_specs=[HBM],
        out_specs=[VMEM] * 2,
        scratch_shapes=[pltpu.SemaphoreType.DMA],
        compiler_params=pltpu.CompilerParams(vmem_limit_bytes=12 << 20),
    )(*in_hbm([array]))


def join(blocks):
    n = len(blocks)
    width = blocks[0].shape[1]

    def body(*refs):
        refs[n][...] = jnp.concatenate([r[...] for r in refs[:n]], axis=0)

    return call(body, jax.ShapeDtypeStruct((n * CAP, width), BF), n)(*blocks)


def streamed(compute, tiles, out_shapes, n_in, smem=0):
    n_out = len(out_shapes)

    def body(*refs):
        ins, outs = refs[:n_in], refs[n_in : n_in + n_out]
        held, sems = refs[n_in + n_out : n_in + 2 * n_out], refs[-1]
        copies = []
        state = None
        for i in range(tiles):
            state, results = compute(ins, i, state)
            for j, (where, value) in enumerate(results):
                held[j][where] = value.astype(BF)
                copy = pltpu.make_async_copy(
                    held[j].at[where], outs[j].at[where], sems.at[i * n_out + j]
                )
                copy.start()
                copies.append(copy)
        for copy in copies:
            copy.wait()

    return pl.pallas_call(
        body,
        out_shape=[jax.ShapeDtypeStruct(shape, BF) for shape in out_shapes],
        in_specs=[SMEM] * smem + [VMEM] * (n_in - smem),
        out_specs=[HBM] * n_out,
        scratch_shapes=[pltpu.VMEM(shape, BF) for shape in out_shapes]
        + [pltpu.SemaphoreType.DMA((tiles * n_out,))],
        compiler_params=pltpu.CompilerParams(vmem_limit_bytes=24 << 20),
    )


OVER_ROWS = (((0,), (0,)), ((), ()))


def unpack(pick, scale, blocks):
    n = len(blocks)
    width = blocks[0].shape[1]
    tok = pick.shape[1]
    lead = [pick] if scale is None else [pick, scale]
    tiles = 4
    cols = width // tiles

    def compute(ins, i, state):
        at = slice(i * cols, (i + 1) * cols)
        chosen = ins[0][...]
        parts = [r[:, at] for r in ins[len(lead) :]]
        if scale is None:
            rows = jnp.concatenate(parts, axis=0)
        else:
            full = jnp.concatenate([p.astype(F32) for p in parts], axis=0) * ins[1][:, 0:1]
            top = full.astype(BF)
            rest = full - top.astype(F32)
            middle = rest.astype(BF)
            low = (rest - middle.astype(F32)).astype(BF)
            rows = jnp.concatenate([top, middle, low], axis=0)
            chosen = jnp.concatenate([chosen, chosen, chosen], axis=0)
        value = lax.dot_general(chosen, rows, OVER_ROWS, preferred_element_type=F32)
        return state, [((slice(None), at), value)]

    kernel = streamed(compute, tiles, [(tok, width)], len(lead) + n)
    return kernel(*lead, *blocks)[0]


def weight_grads(*jobs):
    count = len(jobs)
    shapes = [(left.shape[1], right.shape[1]) for left, right in jobs]
    flat = [v for job in jobs for v in job]
    tiles = 4

    def body(*refs):
        ins, outs = refs[: 2 * count], refs[2 * count : 3 * count]
        held, sems = refs[3 * count : 4 * count], refs[-1]
        copies = []
        for j, (m, n) in enumerate(shapes):
            left, right = ins[2 * j], ins[2 * j + 1]
            for i in range(tiles):
                if m > n:
                    at = (slice(i * m // tiles, (i + 1) * m // tiles), slice(None))
                else:
                    at = (slice(None), slice(i * n // tiles, (i + 1) * n // tiles))
                held[j][at] = lax.dot_general(
                    left[:, at[0]], right[:, at[1]], OVER_ROWS, preferred_element_type=F32
                ).astype(BF)
                copy = pltpu.make_async_copy(held[j].at[at], outs[j].at[at], sems.at[j * tiles + i])
                copy.start()
                copies.append(copy)
        for copy in copies:
            copy.wait()

    return pl.pallas_call(
        body,
        out_shape=[jax.ShapeDtypeStruct(shape, BF) for shape in shapes],
        in_specs=[VMEM] * (2 * count),
        out_specs=[HBM] * count,
        scratch_shapes=[pltpu.VMEM(shape, BF) for shape in shapes]
        + [pltpu.SemaphoreType.DMA((tiles * count,))],
        compiler_params=pltpu.CompilerParams(vmem_limit_bytes=24 << 20),
    )(*flat)


def part_types(n, rows, width, heavy):
    half = n // 2
    starts = {half, n - half + 1} if heavy > 0 else {half, half - 1}
    return [
        jax.ShapeDtypeStruct((rows, width), BF if d in starts else F32) for d in range(n)
    ]


def forward(chunks, w_gate, w_up, w_down, heavy):
    n = len(chunks)
    rows, width = chunks[0].shape
    ff = w_gate.shape[1]
    total = n * rows

    def body(*refs):
        ins, (wg, wu, wd) = refs[:n], refs[n : n + 3]
        all_ref, hidden_ref, act_ref, slope_ref = refs[n + 3 : n + 7]
        outs = refs[n + 7 :]
        for d in range(n):
            all_ref[d * rows : (d + 1) * rows, :] = ins[d][...]
        x = all_ref[...]
        pre_gate = jnp.dot(x, wg[...], preferred_element_type=F32)
        pre_up = jnp.dot(x, wu[...], preferred_element_type=F32)
        logistic = jax.nn.sigmoid(pre_gate)
        activated = pre_gate * logistic
        hidden = (activated * pre_up).astype(BF)
        hidden_ref[...] = hidden
        act_ref[...] = activated
        slope_ref[...] = pre_up * logistic * (1.0 + pre_gate * (1.0 - logistic))
        routed = jnp.dot(hidden, wd[...], preferred_element_type=F32)
        for d in range(n):
            outs[d][...] = routed[d * rows : (d + 1) * rows].astype(outs[d].dtype)

    shape = [
        jax.ShapeDtypeStruct((total, width), BF),
        jax.ShapeDtypeStruct((total, ff), BF),
        jax.ShapeDtypeStruct((total, ff), F32),
        jax.ShapeDtypeStruct((total, ff), F32),
    ] + part_types(n, rows, width, heavy)
    out = call(body, shape, n + 3, limit=24)(*chunks, w_gate, w_up, w_down)
    return out[0], out[1], out[2], out[3], out[4:]


def backward(chunks, activated, slope, gate_t, up_t, down_t, heavy):
    n = len(chunks)
    rows, width = chunks[0].shape
    ff = gate_t.shape[0]
    total = n * rows

    def body(*refs):
        ins, (act_ref, slope_ref, wgt, wut, wdt) = refs[:n], refs[n : n + 5]
        all_ref, dg_ref, du_ref = refs[n + 5 : n + 8]
        outs = refs[n + 8 :]
        for d in range(n):
            all_ref[d * rows : (d + 1) * rows, :] = ins[d][...]
        d_act = jnp.dot(all_ref[...], wdt[...], preferred_element_type=F32)
        d_up = (d_act * act_ref[...]).astype(BF)
        d_gate = (d_act * slope_ref[...]).astype(BF)
        dg_ref[...] = d_gate
        du_ref[...] = d_up
        grads = jnp.dot(d_gate, wgt[...], preferred_element_type=F32)
        grads += jnp.dot(d_up, wut[...], preferred_element_type=F32)
        for d in range(n):
            outs[d][...] = grads[d * rows : (d + 1) * rows].astype(outs[d].dtype)

    shape = [
        jax.ShapeDtypeStruct((total, width), BF),
        jax.ShapeDtypeStruct((total, ff), BF),
        jax.ShapeDtypeStruct((total, ff), BF),
    ] + part_types(n, rows, width, heavy)
    out = call(body, shape, n + 5, limit=24)(*chunks, activated, slope, gate_t, up_t, down_t)
    return out[0], out[1], out[2], out[3:]


def ring_order(n):
    return [i for i in range(0, n, 2)] + [i for i in reversed(range(1, n, 2))]


def shift(value, step):
    n, n_rep = lax.axis_size("ep"), lax.axis_size("rep")
    order = ring_order(n)
    pairs = []
    for r in range(n_rep):
        way = step
        pairs += [
            (order[i] * n_rep + r, order[(i + way) % n] * n_rep + r) for i in range(n)
        ]
    return lax.ppermute(value, ("ep", "rep"), pairs)


def ring_gather(chunk, heavy):
    n = lax.axis_size("ep")
    half = n // 2
    found = {0: chunk}
    ahead = behind = chunk
    for step in range(1, half + 1):
        ahead = shift(ahead, heavy)
        found[(-heavy * step) % n] = ahead
        if step < half:
            behind = shift(behind, -heavy)
            found[(heavy * step) % n] = behind
    return [found[d] for d in range(n)]


def ring_scatter(parts, heavy):
    n = len(parts)
    half = n // 2
    ahead = shift(parts[half], heavy)
    behind = shift(parts[(-heavy * (half - 1)) % n], -heavy)
    for step in range(1, half):
        d = (heavy * (half - step)) % n
        ahead = shift((ahead.astype(F32) + parts[d]).astype(BF), heavy)
        if step < half - 1:
            d = (-heavy * (half - 1 - step)) % n
            behind = shift((behind.astype(F32) + parts[d]).astype(BF), -heavy)
    return parts[0], ahead, behind


def finish(own, ahead, behind, n):
    width = own.shape[1]

    def body(own_ref, ahead_ref, behind_ref, *outs):
        total = own_ref[...] + ahead_ref[...].astype(F32) + behind_ref[...].astype(F32)
        for k in range(n):
            outs[k][...] = total[k * CAP : (k + 1) * CAP].astype(BF)

    shape = [jax.ShapeDtypeStruct((CAP, width), BF)] * n
    return call(body, shape, 3)(own, ahead, behind)


def trade(blocks):
    n = lax.axis_size("rep")
    found = [blocks[0]]
    for k in range(1, n):
        found.append(lax.ppermute(blocks[k], "rep", [(i, i ^ k) for i in range(n)]))
    return found


def local(tokens, expert_ids, route_weights, w_gate, w_up, w_down, cotangent):
    n_rep = lax.axis_size("rep")
    rank_id = lax.axis_index("rep").astype(jnp.int32).reshape(1)
    ids = expert_ids.T
    weights = route_weights.T

    sent, sent_ups, pick, scale = pack(rank_id, ids, weights, tokens, cotangent, n_rep)
    token_rows = join(trade(sent))
    up_rows = join(trade(sent_ups))
    wg, wg_turned = load(w_gate[0])
    wu, wu_turned = load(w_up[0])
    wd, wd_turned = load(w_down[0])
    plain, turned = (wg, wu, wd), (wg_turned, wu_turned, wd_turned)
    token_chunks = ring_gather(token_rows, 1)
    up_chunks = ring_gather(up_rows, -1)
    all_tokens, hidden, activated, slope, routed_parts = forward(token_chunks, *plain, 1)
    routed = ring_scatter(routed_parts, 1)
    all_ups, d_gate, d_up, grad_parts = backward(up_chunks, activated, slope, *turned, -1)
    row_grads = ring_scatter(grad_parts, -1)
    grad_gate, grad_up = weight_grads((all_tokens, d_gate), (all_tokens, d_up))
    (grad_down,) = weight_grads((hidden, all_ups))
    back = trade(finish(*routed, n_rep))
    mixed = unpack(pick, scale, back)
    back = trade(finish(*row_grads, n_rep))
    grad_tokens = unpack(pick, None, back)
    return (mixed, grad_tokens, grad_gate[None], grad_up[None], grad_down[None])


def solution(mesh):
    placed = (
        P(("ep", "rep"), None),
        P(("ep", "rep"), None),
        P(("ep", "rep"), None),
        P("rep", None, "ep"),
        P("rep", None, "ep"),
        P("rep", "ep", None),
        P(("ep", "rep"), None),
    )

    return jax.shard_map(
        local,
        mesh=mesh,
        in_specs=placed,
        out_specs=(
            P(("ep", "rep"), None),
            P(("ep", "rep"), None),
            P("rep", None, "ep"),
            P("rep", None, "ep"),
            P("rep", "ep", None),
        ),
        check_vma=False,
    )
```

```python
import jax
import jax.numpy as jnp
from jax import lax
from jax.experimental import pallas as pl
from jax.experimental.pallas import tpu as pltpu
from jax.sharding import PartitionSpec as P


CAP = 4
BF = jnp.bfloat16
F32 = jnp.float32
VMEM = pl.BlockSpec(memory_space=pltpu.VMEM)
SMEM = pl.BlockSpec(memory_space=pltpu.SMEM)
HBM = pl.BlockSpec(memory_space=pltpu.HBM)


def call(body, out_shape, n_in, limit=12, smem=0):
    return pl.pallas_call(
        body,
        out_shape=out_shape,
        in_specs=[SMEM] * smem + [VMEM] * (n_in - smem),
        out_specs=jax.tree.map(lambda _: VMEM, out_shape),
        compiler_params=pltpu.CompilerParams(vmem_limit_bytes=limit << 20),
    )


def selection(rank_id, ids, n_rep):
    slots = n_rep * CAP
    tok = ids.shape[1]
    row = lax.broadcasted_iota(jnp.int32, (slots, tok), 0)
    expert = jnp.bitwise_xor(rank_id, row // CAP)
    first = ids[0:1, :] == expert
    second = ids[1:2, :] == expert
    member = jnp.logical_or(first, second)
    below = lax.broadcasted_iota(jnp.int32, (tok, tok), 0) < lax.broadcasted_iota(
        jnp.int32, (tok, tok), 1
    )
    earlier = jnp.dot(
        jnp.where(member, 1.0, 0.0).astype(BF),
        jnp.where(below, 1.0, 0.0).astype(BF),
        preferred_element_type=F32,
    )
    chosen = jnp.logical_and(member, earlier == (row % CAP).astype(F32))
    return chosen, first


def slot_weights(chosen, first, weights):
    both = jnp.where(first, weights[0:1, :], weights[1:2, :])
    return jnp.sum(jnp.where(chosen, both, 0.0), axis=1, keepdims=True)


def in_hbm(arrays):
    return [pltpu.with_memory_space_constraint(v, pltpu.HBM) for v in arrays]


def pack(ids, weights, tokens, cotangent, n_rep):
    tok, width = tokens.shape
    slots = n_rep * CAP
    given = [ids, weights, tokens, cotangent]

    def body(*refs):
        ins, outs = refs[:4], refs[4 : 4 + 2 * n_rep]
        pick_ref, scale_ref = refs[4 + 2 * n_rep : 6 + 2 * n_rep]
        held, sems = refs[6 + 2 * n_rep : 10 + 2 * n_rep], refs[-1]
        copies = [
            pltpu.make_async_copy(src, dst, sems.at[i])
            for i, (src, dst) in enumerate(zip(ins, held))
        ]
        for copy in copies:
            copy.start()
        copies[0].wait()
        copies[1].wait()
        chosen, first = selection(lax.axis_index("rep"), held[0][...], n_rep)
        scale = slot_weights(chosen, first, held[1][...])
        pick = jnp.where(chosen, 1.0, 0.0).astype(BF)
        pick_ref[...] = pick
        scale_ref[...] = jnp.broadcast_to(scale, (slots, tok))
        copies[2].wait()
        rows = jnp.dot(pick, held[2][...], preferred_element_type=F32)
        for k in range(n_rep):
            outs[k][...] = rows[k * CAP : (k + 1) * CAP].astype(BF)
        copies[3].wait()
        rows = jnp.dot(pick, held[3][...], preferred_element_type=F32) * scale
        for k in range(n_rep):
            outs[n_rep + k][...] = rows[k * CAP : (k + 1) * CAP].astype(BF)

    out = pl.pallas_call(
        body,
        out_shape=[jax.ShapeDtypeStruct((CAP, width), BF)] * (2 * n_rep)
        + [jax.ShapeDtypeStruct((slots, tok), BF), jax.ShapeDtypeStruct((slots, tok), F32)],
        in_specs=[HBM] * 4,
        out_specs=[VMEM] * (2 * n_rep + 2),
        scratch_shapes=[pltpu.VMEM(v.shape, v.dtype) for v in given]
        + [pltpu.SemaphoreType.DMA((4,))],
        compiler_params=pltpu.CompilerParams(vmem_limit_bytes=12 << 20),
    )(*in_hbm(given))
    return out[:n_rep], out[n_rep : 2 * n_rep], out[-2], out[-1]


def turn(array):
    def body(src, dst):
        dst[...] = src[...].T

    return call(body, jax.ShapeDtypeStruct(array.shape[::-1], array.dtype), 1)(array)


def join(blocks):
    n = len(blocks)
    width = blocks[0].shape[1]

    def body(*refs):
        refs[n][...] = jnp.concatenate([r[...] for r in refs[:n]], axis=0)

    return call(body, jax.ShapeDtypeStruct((n * CAP, width), BF), n)(*blocks)


def streamed(compute, tiles, out_shapes, n_in, smem=0):
    n_out = len(out_shapes)

    def body(*refs):
        ins, outs = refs[:n_in], refs[n_in : n_in + n_out]
        held, sems = refs[n_in + n_out : n_in + 2 * n_out], refs[-1]
        copies = []
        state = None
        for i in range(tiles):
            state, results = compute(ins, i, state)
            for j, (where, value) in enumerate(results):
                held[j][where] = value.astype(BF)
                copy = pltpu.make_async_copy(
                    held[j].at[where], outs[j].at[where], sems.at[i * n_out + j]
                )
                copy.start()
                copies.append(copy)
        for copy in copies:
            copy.wait()

    return pl.pallas_call(
        body,
        out_shape=[jax.ShapeDtypeStruct(shape, BF) for shape in out_shapes],
        in_specs=[SMEM] * smem + [VMEM] * (n_in - smem),
        out_specs=[HBM] * n_out,
        scratch_shapes=[pltpu.VMEM(shape, BF) for shape in out_shapes]
        + [pltpu.SemaphoreType.DMA((tiles * n_out,))],
        compiler_params=pltpu.CompilerParams(vmem_limit_bytes=24 << 20),
    )


OVER_ROWS = (((0,), (0,)), ((), ()))


def unpack(pick, scale, blocks):
    n = len(blocks)
    width = blocks[0].shape[1]
    tok = pick.shape[1]
    lead = [pick] if scale is None else [pick, scale]
    tiles = 4
    cols = width // tiles

    def compute(ins, i, state):
        at = slice(i * cols, (i + 1) * cols)
        chosen = ins[0][...]
        parts = [r[:, at] for r in ins[len(lead) :]]
        if scale is None:
            rows = jnp.concatenate(parts, axis=0)
        else:
            full = jnp.concatenate([p.astype(F32) for p in parts], axis=0) * ins[1][:, 0:1]
            top = full.astype(BF)
            rest = full - top.astype(F32)
            middle = rest.astype(BF)
            low = (rest - middle.astype(F32)).astype(BF)
            rows = jnp.concatenate([top, middle, low], axis=0)
            chosen = jnp.concatenate([chosen, chosen, chosen], axis=0)
        value = lax.dot_general(chosen, rows, OVER_ROWS, preferred_element_type=F32)
        return state, [((slice(None), at), value)]

    kernel = streamed(compute, tiles, [(tok, width)], len(lead) + n)
    return kernel(*lead, *blocks)[0]


def weight_grads(*jobs):
    count = len(jobs)
    shapes = [(left.shape[1], right.shape[1]) for left, right in jobs]
    flat = [v for job in jobs for v in job]
    tiles = 8

    def body(*refs):
        ins, outs = refs[: 2 * count], refs[2 * count : 3 * count]
        held, sems = refs[3 * count : 4 * count], refs[-1]
        copies = []
        for j, (m, n) in enumerate(shapes):
            left, right = ins[2 * j], ins[2 * j + 1]
            for i in range(tiles):
                if m > n:
                    at = (slice(i * m // tiles, (i + 1) * m // tiles), slice(None))
                else:
                    at = (slice(None), slice(i * n // tiles, (i + 1) * n // tiles))
                held[j][at] = lax.dot_general(
                    left[:, at[0]], right[:, at[1]], OVER_ROWS, preferred_element_type=F32
                ).astype(BF)
                copy = pltpu.make_async_copy(held[j].at[at], outs[j].at[at], sems.at[j * tiles + i])
                copy.start()
                copies.append(copy)
        for copy in copies:
            copy.wait()

    return pl.pallas_call(
        body,
        out_shape=[jax.ShapeDtypeStruct(shape, BF) for shape in shapes],
        in_specs=[VMEM] * (2 * count),
        out_specs=[HBM] * count,
        scratch_shapes=[pltpu.VMEM(shape, BF) for shape in shapes]
        + [pltpu.SemaphoreType.DMA((tiles * count,))],
        compiler_params=pltpu.CompilerParams(vmem_limit_bytes=24 << 20),
    )(*flat)


def part_types(n, rows, width, heavy):
    half = n // 2
    starts = {half, n - half + 1} if heavy > 0 else {half, half - 1}
    return [
        jax.ShapeDtypeStruct((rows, width), BF if d in starts else F32) for d in range(n)
    ]


def forward(chunks, w_gate, w_up, w_down, heavy):
    n = len(chunks)
    rows, width = chunks[0].shape
    ff = w_gate.shape[1]
    total = n * rows

    def body(*refs):
        ins, (wg, wu, wd) = refs[:n], refs[n : n + 3]
        all_ref, hidden_ref, act_ref, slope_ref = refs[n + 3 : n + 7]
        outs = refs[n + 7 :]
        for d in range(n):
            all_ref[d * rows : (d + 1) * rows, :] = ins[d][...]
        x = all_ref[...]
        pre_gate = jnp.dot(x, wg[...], preferred_element_type=F32)
        pre_up = jnp.dot(x, wu[...], preferred_element_type=F32)
        logistic = jax.nn.sigmoid(pre_gate)
        activated = pre_gate * logistic
        hidden = (activated * pre_up).astype(BF)
        hidden_ref[...] = hidden
        act_ref[...] = activated
        slope_ref[...] = pre_up * logistic * (1.0 + pre_gate * (1.0 - logistic))
        routed = jnp.dot(hidden, wd[...], preferred_element_type=F32)
        for d in range(n):
            outs[d][...] = routed[d * rows : (d + 1) * rows].astype(outs[d].dtype)

    shape = [
        jax.ShapeDtypeStruct((total, width), BF),
        jax.ShapeDtypeStruct((total, ff), BF),
        jax.ShapeDtypeStruct((total, ff), F32),
        jax.ShapeDtypeStruct((total, ff), F32),
    ] + part_types(n, rows, width, heavy)
    out = call(body, shape, n + 3, limit=24)(*chunks, w_gate, w_up, w_down)
    return out[0], out[1], out[2], out[3], out[4:]


def backward(chunks, activated, slope, gate_t, up_t, down_t, heavy):
    n = len(chunks)
    rows, width = chunks[0].shape
    ff = gate_t.shape[0]
    total = n * rows

    def body(*refs):
        ins, (act_ref, slope_ref, wgt, wut, wdt) = refs[:n], refs[n : n + 5]
        all_ref, dg_ref, du_ref = refs[n + 5 : n + 8]
        outs = refs[n + 8 :]
        for d in range(n):
            all_ref[d * rows : (d + 1) * rows, :] = ins[d][...]
        d_act = jnp.dot(all_ref[...], wdt[...], preferred_element_type=F32)
        d_up = (d_act * act_ref[...]).astype(BF)
        d_gate = (d_act * slope_ref[...]).astype(BF)
        dg_ref[...] = d_gate
        du_ref[...] = d_up
        grads = jnp.dot(d_gate, wgt[...], preferred_element_type=F32)
        grads += jnp.dot(d_up, wut[...], preferred_element_type=F32)
        for d in range(n):
            outs[d][...] = grads[d * rows : (d + 1) * rows].astype(outs[d].dtype)

    shape = [
        jax.ShapeDtypeStruct((total, width), BF),
        jax.ShapeDtypeStruct((total, ff), BF),
        jax.ShapeDtypeStruct((total, ff), BF),
    ] + part_types(n, rows, width, heavy)
    out = call(body, shape, n + 5, limit=24)(*chunks, activated, slope, gate_t, up_t, down_t)
    return out[0], out[1], out[2], out[3:]


def ring_order(n):
    return [i for i in range(0, n, 2)] + [i for i in reversed(range(1, n, 2))]


def shift(value, step):
    n, n_rep = lax.axis_size("ep"), lax.axis_size("rep")
    order = ring_order(n)
    pairs = []
    for r in range(n_rep):
        way = step
        pairs += [
            (order[i] * n_rep + r, order[(i + way) % n] * n_rep + r) for i in range(n)
        ]
    return lax.ppermute(value, ("ep", "rep"), pairs)


def ring_gather(chunk, heavy):
    n = lax.axis_size("ep")
    half = n // 2
    found = {0: chunk}
    ahead = behind = chunk
    for step in range(1, half + 1):
        ahead = shift(ahead, heavy)
        found[(-heavy * step) % n] = ahead
        if step < half:
            behind = shift(behind, -heavy)
            found[(heavy * step) % n] = behind
    return [found[d] for d in range(n)]


def ring_scatter(parts, heavy):
    n = len(parts)
    half = n // 2
    ahead = shift(parts[half], heavy)
    behind = shift(parts[(-heavy * (half - 1)) % n], -heavy)
    for step in range(1, half):
        d = (heavy * (half - step)) % n
        ahead = shift((ahead.astype(F32) + parts[d]).astype(BF), heavy)
        if step < half - 1:
            d = (-heavy * (half - 1 - step)) % n
            behind = shift((behind.astype(F32) + parts[d]).astype(BF), -heavy)
    return parts[0], ahead, behind


def finish(own, ahead, behind, n):
    width = own.shape[1]

    def body(own_ref, ahead_ref, behind_ref, *outs):
        total = own_ref[...] + ahead_ref[...].astype(F32) + behind_ref[...].astype(F32)
        for k in range(n):
            outs[k][...] = total[k * CAP : (k + 1) * CAP].astype(BF)

    shape = [jax.ShapeDtypeStruct((CAP, width), BF)] * n
    return call(body, shape, 3)(own, ahead, behind)


def trade(blocks):
    n = lax.axis_size("rep")
    found = [blocks[0]]
    for k in range(1, n):
        found.append(lax.ppermute(blocks[k], "rep", [(i, i ^ k) for i in range(n)]))
    return found


def local(tokens, expert_ids, route_weights, w_gate, w_up, w_down, cotangent):
    n_rep = lax.axis_size("rep")
    ids = expert_ids.T
    weights = route_weights.T

    sent, sent_ups, pick, scale = pack(ids, weights, tokens, cotangent, n_rep)
    token_rows = join(trade(sent))
    up_rows = join(trade(sent_ups))
    plain = [w_gate[0], w_up[0], w_down[0]]
    turned = [turn(w) for w in plain]
    token_chunks = ring_gather(token_rows, 1)
    up_chunks = ring_gather(up_rows, -1)
    all_tokens, hidden, activated, slope, routed_parts = forward(token_chunks, *plain, 1)
    routed = ring_scatter(routed_parts, 1)
    all_ups, d_gate, d_up, grad_parts = backward(up_chunks, activated, slope, *turned, -1)
    row_grads = ring_scatter(grad_parts, -1)
    grad_gate, grad_up = weight_grads((all_tokens, d_gate), (all_tokens, d_up))
    (grad_down,) = weight_grads((hidden, all_ups))
    back = trade(finish(*routed, n_rep))
    mixed = unpack(pick, scale, back)
    back = trade(finish(*row_grads, n_rep))
    grad_tokens = unpack(pick, None, back)
    return (mixed, grad_tokens, grad_gate[None], grad_up[None], grad_down[None])


def solution(mesh):
    placed = (
        P(("ep", "rep"), None),
        P(("ep", "rep"), None),
        P(("ep", "rep"), None),
        P("rep", None, "ep"),
        P("rep", None, "ep"),
        P("rep", "ep", None),
        P(("ep", "rep"), None),
    )

    return jax.shard_map(
        local,
        mesh=mesh,
        in_specs=placed,
        out_specs=(
            P(("ep", "rep"), None),
            P(("ep", "rep"), None),
            P("rep", None, "ep"),
            P("rep", None, "ep"),
            P("rep", "ep", None),
        ),
        check_vma=False,
    )
```
